32 devices in a mesh: groups: 2 (over x), seq: 16 (over z, y, core).
Axes of the slice: x: 2, y: 2, z: 4, core: 2. Of those that a mesh axis runs over, the one named last changes fastest.
Arguments:
- queries: bfloat16 [16384, 1536], P(('groups', 'seq')), parts along dimension 0, may hold values from -5 to 5
- key_vectors: bfloat16 [16384, 1536], P(('groups', 'seq')), parts along dimension 0, may hold values from -5 to 5
- value_vectors: bfloat16 [16384, 1536], P(('groups', 'seq')), parts along dimension 0, may hold values from -6 to 6
- hidden: bfloat16 [16384, 1536], P(('groups', 'seq')), parts along dimension 0, may hold values from -6 to 6
- out_weight: bfloat16 [1536, 1536], replicated, may hold values from -0.15625 to 0.15625
- conv_weight: bfloat16 [31, 1536], replicated, may hold values from -1 to 1
- cotangent: bfloat16 [16384, 1536], P(('groups', 'seq')), parts along dimension 0, may hold values from -6 to 6
- valid_mask: int32 [16384], P(('groups', 'seq')), parts along dimension 0, may hold values from 0 to 1, as said below
Outputs:
- grad_queries: bfloat16 [16384, 1536], P(('groups', 'seq')), parts along dimension 0
- grad_keys: bfloat16 [16384, 1536], P(('groups', 'seq')), parts along dimension 0
- grad_values: bfloat16 [16384, 1536], P(('groups', 'seq')), parts along dimension 0
- grad_hidden: bfloat16 [16384, 1536], P(('groups', 'seq')), parts along dimension 0
- grad_out_weight: float32 [3072, 1536], P(('groups', 'seq')), parts along dimension 0
- grad_conv_weight: float32 [62, 1536], P('groups'), parts along dimension 0
The draws below stay inside these ranges and needn't reach their ends.
There are 2 independent parts, one for each index of `groups`. The reference program is written for one: setup_inputs(seed, part) draws one part's arguments, and reference() takes and returns one part's arrays. A program takes and returns all parts, laid end to end along the dimension named above; an argument that names none is the same for every part. Nothing has to cross between parts.
Inputs may be any that keep to these rules, and one draw needn't show every extreme that they name: valid_mask is 1 on the frames before a length and 0 from it on; the length lies between 8065 and 8191.
All inputs are finite; a program needn't handle non-finite values.
Results may differ from the reference program's by a relative error of at most 0.019.
Values may be sent and summed in bfloat16 or wider, within the bound.
No kernel may reach another device: no remote copies, remote signals or barrier semaphores. Data moves between devices by JAX's collectives and lax.ppermute only.
A program may use at most 128 MiB of HBM per device.

```python
import math
import jax
import jax.numpy as jnp
from jax import lax

D = 1536
HEADS = 16
HEAD = 96
KERNEL = 31
BLOCK = 128
FRAMES = 8192


def draw_queries(key, part):
    field_key = jax.random.fold_in(key, 101)
    field = jnp.clip(jax.random.normal(field_key, (FRAMES, D), jnp.float32), -4.0, 4.0)
    return field.astype(jnp.bfloat16)


def draw_key_vectors(key, part):
    field_key = jax.random.fold_in(key, 202)
    field = jnp.clip(jax.random.normal(field_key, (FRAMES, D), jnp.float32), -4.0, 4.0)
    return field.astype(jnp.bfloat16)


def draw_valid_mask(key, part):
    cut_frames = jax.random.randint(jax.random.fold_in(key, 303), (), 1, BLOCK)
    length = FRAMES - cut_frames
    positions = jnp.arange(FRAMES, dtype=jnp.int32)
    return (positions < length).astype(jnp.int32)


def block_scale(key, dims, shards, low, high):
    loudness, own = 1.0, jax.random.fold_in(key, 6)
    for axis_at, parts in shards:
        steps = jnp.exp(jax.random.uniform(jax.random.fold_in(own, axis_at), (parts,), jnp.float32, low / len(shards), high / len(shards)))
        loudness = loudness * jnp.repeat(steps, dims[axis_at] // parts).reshape([-1 if axis == axis_at else 1 for axis in range(len(dims))])
    return loudness


def gaussian(own_key, shape, scale, reach, split=(), kind=jnp.bfloat16):
    entries = jax.random.normal(own_key, shape, jnp.float32) * scale
    if len(split) > 0:
        entries = block_scale(own_key, shape, split, -0.22, 0.18) * entries
    return jnp.clip(entries, min=-reach, max=reach).astype(kind)


def setup_inputs(seed: int = 0, part: int = 0) -> dict:
    seeds = jax.random.split(jax.random.key(seed), 9)
    part_splits = jax.random.split(jax.random.fold_in(seeds[8], part), 9)
    queries = draw_queries(jax.random.fold_in(jax.random.fold_in(seeds[8], part), 71), part)
    key_vectors = draw_key_vectors(jax.random.fold_in(jax.random.fold_in(seeds[8], part), 71), part)
    value_vectors = gaussian(part_splits[2], (FRAMES, D), 1.0, 6.0, ((0, 16),))
    hidden = gaussian(part_splits[3], (FRAMES, D), 1.0, 6.0, ((0, 16),))
    out_weight = gaussian(seeds[4], (D, D), D ** -0.5, 0.15625)
    conv_weight = gaussian(seeds[5], (KERNEL, D), KERNEL ** -0.5, 1.0)
    cotangent = gaussian(part_splits[6], (FRAMES, D), 1.0, 6.0, ((0, 16),))
    valid_mask = draw_valid_mask(jax.random.fold_in(jax.random.fold_in(seeds[8], part), 71), part)
    return dict(queries=queries, key_vectors=key_vectors, value_vectors=value_vectors, hidden=hidden, out_weight=out_weight, conv_weight=conv_weight, cotangent=cotangent, valid_mask=valid_mask)


def block_grads(operands):
    query_blk, key_win, value_win, mask_win, grad_blk = operands
    score_scale = 1.0 / math.sqrt(HEAD)
    query_f = query_blk.astype(jnp.float32).reshape(BLOCK, HEADS, HEAD)
    key_f = key_win.astype(jnp.float32).reshape(2 * BLOCK, HEADS, HEAD)
    value_f = value_win.astype(jnp.float32).reshape(2 * BLOCK, HEADS, HEAD)
    grad_f = grad_blk.astype(jnp.float32).reshape(BLOCK, HEADS, HEAD)
    scores = jnp.einsum('qhd,khd->hqk', query_f, key_f) * score_scale
    allowed = (mask_win == 1)[None, None, :]
    row_max = lax.optimization_barrier(jnp.max(jnp.where(allowed, scores, -1e+30), axis=-1, keepdims=True))
    weights_raw = jnp.where(allowed, jnp.exp(scores - row_max), 0.0)
    probs = weights_raw / lax.optimization_barrier(jnp.sum(weights_raw, axis=-1, keepdims=True))
    probs_b = lax.optimization_barrier(probs.astype(jnp.bfloat16)).astype(jnp.float32)
    attended = jnp.einsum('hqk,khd->qhd', probs_b, value_f).astype(jnp.bfloat16)
    dprobs = jnp.einsum('qhd,khd->hqk', grad_f, value_f)
    delta = jnp.einsum('qhd,qhd->hq', grad_f, attended.astype(jnp.float32))[..., None]
    grad_scores = (probs * (dprobs - delta) * score_scale).astype(jnp.bfloat16)
    grad_scores = lax.optimization_barrier(grad_scores).astype(jnp.float32)
    grad_query = jnp.einsum('hqk,khd->qhd', grad_scores, key_f)
    grad_key = jnp.einsum('hqk,qhd->khd', grad_scores, query_f)
    grad_value = jnp.einsum('hqk,qhd->khd', probs_b, grad_f)
    return (attended.reshape(BLOCK, D), grad_query.reshape(BLOCK, D), grad_key.reshape(2 * BLOCK, D), grad_value.reshape(2 * BLOCK, D))

def reference(queries, key_vectors, value_vectors, hidden, out_weight, conv_weight, cotangent, valid_mask):
    rim_rows = KERNEL - 1
    block_count = FRAMES // BLOCK
    upstream = cotangent.astype(jnp.float32)
    conv_taps = conv_weight.astype(jnp.float32)
    padded = jnp.concatenate([upstream, jnp.zeros((rim_rows, D), jnp.float32)], axis=0)
    running = jnp.zeros((FRAMES, D), jnp.float32)
    for offset in range(KERNEL):
        running = running + conv_taps[offset] * padded[offset:offset + FRAMES]
    grad_hidden = running.astype(jnp.bfloat16)
    hidden_pad = jnp.concatenate([jnp.zeros((rim_rows, D), jnp.float32), hidden.astype(jnp.float32)], axis=0)
    tap_rows = []
    for offset in range(KERNEL):
        tap_rows.append(lax.optimization_barrier(jnp.sum(hidden_pad[rim_rows - offset:rim_rows - offset + FRAMES] * upstream, axis=0)))
    grad_conv_weight = jnp.stack(tap_rows, axis=0)
    grad_attended = jnp.dot(grad_hidden, out_weight.T, preferred_element_type=jnp.float32).astype(jnp.bfloat16)
    key_ext = jnp.concatenate([jnp.zeros((BLOCK, D), jnp.bfloat16), key_vectors], axis=0)
    value_ext = jnp.concatenate([jnp.zeros((BLOCK, D), jnp.bfloat16), value_vectors], axis=0)
    mask_ext = jnp.concatenate([jnp.zeros((BLOCK,), jnp.int32), valid_mask.astype(jnp.int32)], axis=0)
    key_windows = jnp.concatenate([key_ext[:FRAMES].reshape(block_count, BLOCK, D), key_ext[BLOCK:].reshape(block_count, BLOCK, D)], axis=1)
    value_windows = jnp.concatenate([value_ext[:FRAMES].reshape(block_count, BLOCK, D), value_ext[BLOCK:].reshape(block_count, BLOCK, D)], axis=1)
    mask_windows = jnp.concatenate([mask_ext[:FRAMES].reshape(block_count, BLOCK), mask_ext[BLOCK:].reshape(block_count, BLOCK)], axis=1)
    attended, grad_query, grad_key_win, grad_value_win = lax.map(block_grads, (queries.reshape(block_count, BLOCK, D), key_windows, value_windows, mask_windows, grad_attended.reshape(block_count, BLOCK, D)))
    zero_block = jnp.zeros((1, BLOCK, D), jnp.float32)
    grad_keys = grad_key_win[:, BLOCK:] + jnp.concatenate([grad_key_win[1:, :BLOCK], zero_block], axis=0)
    grad_values = grad_value_win[:, BLOCK:] + jnp.concatenate([grad_value_win[1:, :BLOCK], zero_block], axis=0)
    attended_rows = attended.reshape(FRAMES, D)
    grad_out_weight = jnp.dot(attended_rows.T, grad_hidden, preferred_element_type=jnp.float32)
    return (grad_query.reshape(FRAMES, D).astype(jnp.bfloat16), grad_keys.reshape(FRAMES, D).astype(jnp.bfloat16), grad_values.reshape(FRAMES, D).astype(jnp.bfloat16), grad_hidden, grad_out_weight, grad_conv_weight)
```

```python
import math

import jax
import jax.numpy as jnp
from jax import lax
from jax.experimental import pallas as pl
from jax.experimental.pallas import tpu as pltpu
from jax.sharding import PartitionSpec as P

HEADS = 16
KERNEL = 31
BLOCK = 128
LANES = 128
HALO = 32
CHUNK = 64
AXIS = "seq"
F32 = jnp.float32
BF16 = jnp.bfloat16


def shifted(value, steps):
    count = lax.axis_size(AXIS)
    initial, last = (max(0, -steps), min(count, count - steps))
    return lax.ppermute(value, AXIS, [(s, s + steps) for s in range(initial, last)])


def exchanged(value, bit):
    count = lax.axis_size(AXIS)
    return lax.ppermute(value, AXIS, [(i, i ^ (1 << bit)) for i in range(count)])


def dot(a, b, ca, cb):
    return lax.dot_general(a, b, (((ca,), (cb,)), ((), ())), preferred_element_type=F32)


def conv_kernel(cot_ref, next_ref, hid_ref, taps_ref, gh_ref, gw_ref, cs, wb, acc_w):
    rows, width = cot_ref.shape
    for tile in range(width // LANES):
        lanes = slice(tile * LANES, (tile + 1) * LANES)
        cs[:rows, :] = cot_ref[:, lanes].astype(F32)
        cs[rows:, :] = next_ref[:, lanes].astype(F32)
        taps = taps_ref[:, lanes].astype(F32)
        for m in range(KERNEL):
            wb[m] = jnp.broadcast_to(taps[m : m + 1], (8, LANES))
        acc_w[...] = jnp.zeros_like(acc_w)

        def step(i, carry, lanes=lanes):
            base = pl.multiple_of(i * CHUNK, CHUNK)
            count = CHUNK // 8
            hid = hid_ref[pl.ds(base, CHUNK), lanes].astype(F32)
            hid = [hid[8 * j : 8 * j + 8] for j in range(count)]
            out = [None] * count
            for r in range(8):
                offsets = list(range(r, KERNEL, 8))
                c = [cs[pl.ds(base + r + 8 * j, 8), :] for j in range(count + len(offsets) - 1)]
                for a, m in enumerate(offsets):
                    tap = wb[m]
                    prods = []
                    for j in range(count):
                        term = tap * c[j + a]
                        out[j] = term if out[j] is None else out[j] + term
                        prods.append(hid[j] * c[j + a])
                    while len(prods) > 1:
                        prods = [prods[k] + prods[k + 1] for k in range(0, len(prods), 2)]
                    acc_w[m] += prods[0]
            gh_ref[pl.ds(base, CHUNK), lanes] = jnp.concatenate(out, axis=0).astype(BF16)
            return carry

        lax.fori_loop(0, rows // CHUNK, step, 0)
        gw_ref[:KERNEL, lanes] = jnp.sum(acc_w[...], axis=1).astype(BF16)
        gw_ref[KERNEL:, lanes] = jnp.zeros((gw_ref.shape[0] - KERNEL, LANES), BF16)


def convolution(cotangent, cot_next, hidden, conv_weight):
    rows, features = cotangent.shape
    width = 3 * LANES
    col = lambda g: (0, g)
    return pl.pallas_call(
        conv_kernel,
        name="conv",
        grid=(features // width,),
        in_specs=[
            pl.BlockSpec((rows, width), col),
            pl.BlockSpec((HALO, width), col),
            pl.BlockSpec((rows, width), col),
            pl.BlockSpec((KERNEL, width), col),
        ],
        out_specs=[pl.BlockSpec((rows, width), col), pl.BlockSpec((HALO, width), col)],
        out_shape=[
            jax.ShapeDtypeStruct((rows, features), BF16),
            jax.ShapeDtypeStruct((HALO, features), BF16),
        ],
        scratch_shapes=[
            pltpu.VMEM((rows + HALO, LANES), F32),
            pltpu.VMEM((KERNEL, 8, LANES), F32),
            pltpu.VMEM((KERNEL, 8, LANES), F32),
        ],
    )(cotangent, cot_next, hidden, conv_weight)


def pair_masks(pair, head, dtype):
    at = lax.broadcasted_iota(jnp.int32, (1, 2 * LANES), 1)
    low = pair * (2 * head - LANES)
    first = (at >= low) & (at < low + head)
    second = (at >= low + head) & (at < low + 2 * head)
    return first.astype(F32).astype(dtype), second.astype(F32).astype(dtype)


def window(pair):
    return slice(pair * LANES, pair * LANES + 2 * LANES)


def key_window(ctx_ref, which, ref, b, pair):
    win = window(pair)
    if b == 0:
        return jnp.concatenate([ctx_ref[which, :, win], ref[:BLOCK, win]], axis=0)
    return ref[(b - 1) * BLOCK : (b + 1) * BLOCK, win]


def stacked(ref, b, pair, masks):
    rows = ref[b * BLOCK : (b + 1) * BLOCK, window(pair)]
    return jnp.concatenate([rows * masks[0], rows * masks[1]], axis=0)


def forward_kernel(q_ref, k_ref, v_ref, ctx_ref, bias_ref, att_ref, p_ref):
    rows, width = q_ref.shape
    head = width // 4
    factor = math.log2(math.e) / math.sqrt(head)
    for pair in range(2):
        masks = pair_masks(pair, head, BF16)
        low = pair * (2 * head - LANES)
        for b in range(rows // BLOCK):
            keys = key_window(ctx_ref, 0, k_ref, b, pair)
            values = key_window(ctx_ref, 1, v_ref, b, pair)
            bias = bias_ref[b * BLOCK : (b + 2) * BLOCK, :]
            scores = dot(keys, stacked(q_ref, b, pair, masks), 1, 1)
            scores = scores * factor + jnp.concatenate([bias, bias], axis=1)
            top = jnp.max(scores, axis=0, keepdims=True)
            weights = jnp.exp2(scores - top)
            total = jnp.sum(weights, axis=0, keepdims=True)
            probs = (weights * (1.0 / total)).astype(BF16)
            p_ref[b, pair] = probs
            out = dot(values, probs, 0, 0).astype(BF16)
            cols = slice(b * BLOCK, (b + 1) * BLOCK)
            at = 2 * head * pair
            att_ref[at : at + head, cols] = out[low : low + head, :BLOCK]
            att_ref[at + head : at + 2 * head, cols] = out[low + head : low + 2 * head, BLOCK:]


def forward_attention(queries, keys, values, context, bias):
    rows, features = queries.shape
    width = 4 * (features // HEADS)
    assert width == 3 * LANES
    blocks = rows // BLOCK
    col = lambda g: (0, g)
    return pl.pallas_call(
        forward_kernel,
        name="forward",
        grid=(features // width,),
        in_specs=[
            pl.BlockSpec((rows, width), col),
            pl.BlockSpec((rows, width), col),
            pl.BlockSpec((rows, width), col),
            pl.BlockSpec((2, BLOCK, width), lambda g: (0, 0, g)),
            pl.BlockSpec((rows + BLOCK, LANES), lambda g: (0, 0)),
        ],
        out_specs=[
            pl.BlockSpec((width, rows), lambda g: (g, 0)),
            pl.BlockSpec((blocks, 2, 2 * BLOCK, 2 * BLOCK), lambda g: (0, g, 0, 0)),
        ],
        out_shape=[
            jax.ShapeDtypeStruct((features, rows), BF16),
            jax.ShapeDtypeStruct((blocks, HEADS // 2, 2 * BLOCK, 2 * BLOCK), BF16),
        ],
    )(queries, keys, values, context, bias)


def backward_kernel(
    gh_ref, w_ref, q_ref, k_ref, v_ref, ctx_ref, p_ref, gq_ref, gk_ref, gv_ref, back_ref, last_ref, ga
):
    rows, width = q_ref.shape
    head = width // 4
    scale = 1.0 / math.sqrt(head)
    blocks = rows // BLOCK
    ga[...] = dot(gh_ref[...], w_ref[...], 1, 1).astype(BF16)

    def merged(parts):
        first, second = parts
        return jnp.concatenate(
            [first[:, :LANES], first[:, LANES:] + second[:, :LANES], second[:, LANES:]], axis=1
        )

    above_k = above_v = None
    for b in range(blocks):
        gq, gk, gv = [], [], []
        for pair in range(2):
            masks = pair_masks(pair, head, BF16)
            masks_f = pair_masks(pair, head, F32)
            keys = key_window(ctx_ref, 0, k_ref, b, pair)
            values = key_window(ctx_ref, 1, v_ref, b, pair)
            q2 = stacked(q_ref, b, pair, masks)
            g2 = stacked(ga, b, pair, masks)
            probs = p_ref[b, pair]
            dprobs = dot(values, g2, 1, 1)
            probs_f = probs.astype(F32)
            weighted = probs_f * dprobs
            delta = jnp.sum(weighted, axis=0, keepdims=True)
            dscores = (weighted - probs_f * delta).astype(BF16)
            gv.append(dot(probs, g2, 1, 0))
            gk.append(dot(dscores, q2, 1, 0))
            both = dot(dscores, keys, 0, 0)
            gq.append(both[:BLOCK] * masks_f[0] + both[BLOCK:] * masks_f[1])
        gq_ref[b * BLOCK : (b + 1) * BLOCK, :] = (merged(gq) * scale).astype(BF16)
        gk = merged(gk) * scale
        gv = merged(gv)
        if b == 0:
            back_ref[0] = gk[:BLOCK].astype(BF16)
            back_ref[1] = gv[:BLOCK].astype(BF16)
        else:
            at = slice((b - 1) * BLOCK, b * BLOCK)
            gk_ref[at, :] = (above_k + gk[:BLOCK]).astype(BF16)
            gv_ref[at, :] = (above_v + gv[:BLOCK]).astype(BF16)
        above_k, above_v = gk[BLOCK:], gv[BLOCK:]
    at = slice((blocks - 1) * BLOCK, blocks * BLOCK)
    gk_ref[at, :] = above_k.astype(BF16)
    gv_ref[at, :] = above_v.astype(BF16)
    last_ref[0] = above_k
    last_ref[1] = above_v


def backward_attention(grad_hidden, out_weight, queries, keys, values, context, probs):
    rows, features = queries.shape
    width = 4 * (features // HEADS)
    blocks = rows // BLOCK
    col = lambda g: (0, g)
    rim = pl.BlockSpec((2, BLOCK, width), lambda g: (0, 0, g))
    wide = pl.BlockSpec((rows, width), col)
    return pl.pallas_call(
        backward_kernel,
        name="backward",
        grid=(features // width,),
        in_specs=[
            pl.BlockSpec((rows, features), lambda g: (0, 0)),
            pl.BlockSpec((width, features), lambda g: (g, 0)),
            wide,
            wide,
            wide,
            rim,
            pl.BlockSpec((blocks, 2, 2 * BLOCK, 2 * BLOCK), lambda g: (0, g, 0, 0)),
        ],
        out_specs=[wide, wide, wide, rim, rim],
        out_shape=[
            jax.ShapeDtypeStruct((rows, features), BF16),
            jax.ShapeDtypeStruct((rows, features), BF16),
            jax.ShapeDtypeStruct((rows, features), BF16),
            jax.ShapeDtypeStruct((2, BLOCK, features), BF16),
            jax.ShapeDtypeStruct((2, BLOCK, features), F32),
        ],
        scratch_shapes=[pltpu.VMEM((rows, width), BF16)],
    )(grad_hidden, out_weight, queries, keys, values, context, probs)


def finish_kernel(gk_in, gv_in, last_ref, back_ref, gk_ref, gv_ref):
    gk_ref[...] = (last_ref[0] + back_ref[0].astype(F32)).astype(BF16)
    gv_ref[...] = (last_ref[1] + back_ref[1].astype(F32)).astype(BF16)


def finish(gk, gv, last, back):
    rows, features = gk.shape
    rim = pl.BlockSpec((2, BLOCK, features), lambda i: (0, 0, 0))
    end = pl.BlockSpec((BLOCK, features), lambda i: (rows // BLOCK - 1, 0))
    whole = pl.BlockSpec(memory_space=pl.ANY)
    return pl.pallas_call(
        finish_kernel,
        name="finish",
        grid=(1,),
        in_specs=[whole, whole, rim, rim],
        out_specs=[end, end],
        out_shape=[jax.ShapeDtypeStruct(gk.shape, BF16), jax.ShapeDtypeStruct(gv.shape, BF16)],
        input_output_aliases={0: 0, 1: 1},
    )(gk, gv, last, back)


def place(block, order):
    at = 0
    for bit in order:
        at = 2 * at + ((block >> bit) & 1)
    return at


def partial_kernel(order, bit_ref, att_ref, gh_ref, *refs):
    taps, (keep_ref, send_ref, both) = refs[:-3], refs[-3:]
    count = 1 << len(order)
    features = att_ref.shape[0]
    size = features // count
    step = features // 4
    for part in range(4):
        out = dot(att_ref[part * step : (part + 1) * step, :], gh_ref[...], 1, 0).astype(BF16)
        for i in range(step // size):
            half, at = divmod(place(part * (step // size) + i, order), count // 2)
            both[half, at * size : (at + 1) * size, :] = out[i * size : (i + 1) * size]
    mine = bit_ref[0]
    keep_ref[...] = both[mine]
    send_ref[: features // 2, :] = both[1 - mine]
    for i, ref in enumerate(taps):
        at = features // 2 + i * HALO
        send_ref[at : at + HALO, :] = ref[...]


def partial_product(attended_t, grad_hidden, first_col, cols, order, taps=None):
    features, rows = attended_t.shape
    width = 2 * LANES
    count = 1 << len(order)
    assert cols % width == 0 and (features // 4) % (features // count) == 0
    bit = ((lax.axis_index(AXIS) >> order[0]) & 1).astype(jnp.int32).reshape(1)
    extra, args = [], []
    if taps is not None:
        for part in range(features // cols):
            extra.append(pl.BlockSpec((HALO, width), lambda j, s, part=part: (0, part * (cols // width) + j)))
            args.append(taps)
    height = features // 2 + HALO * len(extra)

    def kernel(*refs):
        partial_kernel(order, *refs)

    return pl.pallas_call(
        kernel,
        name="partial",
        grid_spec=pltpu.PrefetchScalarGridSpec(
            num_scalar_prefetch=1,
            grid=(cols // width,),
            in_specs=[
                pl.BlockSpec((features, rows), lambda j, s: (0, 0)),
                pl.BlockSpec((rows, width), lambda j, s: (0, first_col // width + j)),
                *extra,
            ],
            out_specs=[
                pl.BlockSpec((features // 2, width), lambda j, s: (0, j)),
                pl.BlockSpec((height, width), lambda j, s: (0, j)),
            ],
            scratch_shapes=[pltpu.VMEM((2, features // 2, width), BF16)],
        ),
        out_shape=[
            jax.ShapeDtypeStruct((features // 2, cols), BF16),
            jax.ShapeDtypeStruct((height, cols), BF16),
        ],
    )(bit, attended_t, grad_hidden, *args)


def halves(value, bit):
    mine = (lax.axis_index(AXIS) >> bit) & 1
    value = value.reshape((2, value.shape[0] // 2) + value.shape[1:])
    return (
        lax.dynamic_index_in_dim(value, mine, 0, False),
        lax.dynamic_index_in_dim(value, 1 - mine, 0, False),
    )


def reduce_rows(keep, send, order, taps=None):
    for step, bit in enumerate(order):
        got = exchanged(send, bit)
        rows = keep.shape[0]
        total = keep.astype(F32) + got[:rows].astype(F32)
        if taps is not None:
            taps = taps.astype(BF16).astype(F32) + got[rows:].astype(F32)
        if step + 1 == len(order):
            return total, taps
        keep, send = halves(total.astype(BF16), order[step + 1])
        if taps is not None:
            send = jnp.concatenate([send, taps.astype(BF16)], axis=0)


def per_device(
    queries, key_vectors, value_vectors, hidden, out_weight, conv_weight, cotangent, valid_mask
):
    frames, features = queries.shape
    count = lax.axis_size(AXIS)
    bits = count.bit_length() - 1
    assert count == 1 << bits and bits >= 2
    order_a = list(range(bits))
    order_b = [0, *range(2, bits), 1]

    cot_next = shifted(cotangent[:HALO], -1)
    context = shifted(jnp.stack([key_vectors[frames - BLOCK :], value_vectors[frames - BLOCK :]]), 1)
    grad_hidden, taps = convolution(cotangent, cot_next, hidden, conv_weight)

    has_context = jnp.broadcast_to((lax.axis_index(AXIS) > 0).astype(jnp.int32), (BLOCK,))
    allowed = jnp.concatenate([has_context, valid_mask]) == 1
    bias = jnp.broadcast_to(jnp.where(allowed, 0.0, -1e30).astype(F32)[:, None], (frames + BLOCK, LANES))
    attended_t, probs = forward_attention(queries, key_vectors, value_vectors, context, bias)

    cols = features // 2
    keep_a, send_a = partial_product(attended_t, grad_hidden, 0, cols, order_a)
    keep_b, send_b = partial_product(attended_t, grad_hidden, cols, cols, order_b, taps)
    own_taps = jnp.concatenate([taps[:, :cols], taps[:, cols:]], axis=0)

    gq, gk, gv, back, last = backward_attention(
        grad_hidden, out_weight, queries, key_vectors, value_vectors, context, probs
    )
    gk, gv = finish(gk, gv, last, shifted(back, -1))

    rows_a, _ = reduce_rows(keep_a, send_a, order_a)
    rows_b, sums = reduce_rows(keep_b, send_b, order_b, own_taps)
    grad_out_weight = jnp.concatenate([rows_a, rows_b], axis=1)
    grad_conv_weight = jnp.concatenate([sums[:KERNEL], sums[HALO : HALO + KERNEL]], axis=1)
    return gq, gk, gv, grad_hidden, grad_out_weight, grad_conv_weight


def solution(mesh):
    rows = P(("groups", AXIS), None)
    in_specs = (rows, rows, rows, rows, P(), P(), rows, P(("groups", AXIS)))
    out_specs = (rows, rows, rows, rows, rows, P("groups", None))
    return jax.shard_map(
        per_device, mesh=mesh, in_specs=in_specs, out_specs=out_specs, check_vma=False
    )
```
